32 devices in a mesh: rows: 16 (over z, y, core), cent: 2 (over x).
Axes of the slice: x: 2, y: 2, z: 4, core: 2. Of those that a mesh axis runs over, the one named last changes fastest.
Arguments:
- vectors: bfloat16 [32768, 1024], P('rows'), may hold values from -40 to 40
- centroids: bfloat16 [1024, 4096], P('rows', 'cent'), may hold values from -8 to 8
Outputs:
- centroid_sums: float32 [1024, 4096], P('rows', 'cent')
The draws below stay inside these ranges and needn't reach their ends.
All inputs are finite; a program needn't handle non-finite values.
Results may differ from the reference program's by a relative error of at most 0.0017.
Values may be sent and summed in bfloat16 or wider, within the bound.
A program may use at most 64 MiB of HBM per device.

```python
import math
import jax
import jax.numpy as jnp
from jax import lax

D = 1024
K = 4096
ITERS = 3
N = 32768


def column_norms(key):
    return jnp.exp(jax.random.uniform(jax.random.fold_in(key, 13), (K,), jnp.float32, math.log(0.5), math.log(2.0)))


def centroid_table(key):
    base = jnp.clip(jax.random.normal(jax.random.fold_in(key, 11), (D, K), jnp.float32), -4.0, 4.0)
    return base * column_norms(key)[None, :]


def draw_centroids(key, part):
    return centroid_table(key).astype(jnp.bfloat16)


def draw_vectors(key, part):
    base = jnp.clip(jax.random.normal(jax.random.fold_in(key, 23), (N, D), jnp.float32), -6.0, 6.0)
    return jnp.clip(base, -40.0, 40.0).astype(jnp.bfloat16)


def setup_inputs(seed: int = 0) -> dict:
    seeds = jax.random.split(jax.random.key(seed), 3)
    vectors = draw_vectors(jax.random.fold_in(seeds[2], 71), 0)
    centroids = draw_centroids(jax.random.fold_in(seeds[2], 71), 0)
    return {"vectors": vectors, "centroids": centroids}


sharpness = 3.0

def reference(vectors, centroids):
    scores = jnp.dot(vectors, centroids, preferred_element_type=jnp.float32) * (sharpness / math.sqrt(D))
    row_top = lax.optimization_barrier(jnp.max(scores, axis=1, keepdims=True))
    numerator = jnp.exp(scores - row_top)
    balanced = numerator / lax.optimization_barrier(jnp.sum(numerator, axis=1, keepdims=True))
    target = N / K
    for iteration in range(ITERS):
        column_mass = lax.optimization_barrier(jnp.sum(balanced, axis=0))
        column_scale = target / column_mass
        balanced = balanced * column_scale[None, :]
        balanced = balanced / lax.optimization_barrier(jnp.sum(balanced, axis=1, keepdims=True))
    weights = balanced.astype(jnp.bfloat16)
    summed = lax.dot_general(vectors, weights, (((0,), (0,)), ((), ())), preferred_element_type=jnp.float32)
    return summed * (K / N)
```

```python
import functools
import math

import jax
import jax.numpy as jnp
from jax import lax
from jax.experimental import pallas as pl
from jax.experimental.pallas import tpu as pltpu
from jax.sharding import PartitionSpec as P

ITERS = 3
SHARPNESS = 3.0
MESH = pl.DeviceIdType.MESH
LANES = 128


def position_of(row, ring):
    chips = ring // 2
    chip, core = row // 2, row % 2
    far, near = chip // 2, chip % 2
    place = far + near * (chips - 1 - 2 * far)
    return place * 2 + core


def row_at(position, ring):
    chips = ring // 2
    place, core = position // 2, position % 2
    half = chips // 2
    near = place // half
    far = place + near * (chips - 1 - 2 * place)
    return (far * 2 + near) * 2 + core


def kernel(ring, groups, total_rows, columns_total, vec_ref, cen_ref, out_ref, cen_full, vec_t, bal, wts, rows_b,
           part, row_x, col_x, sum_in, ag_send, ag_recv, row_send, row_recv, col_send, col_recv, rs_send, rs_recv):
    rows, width = vec_ref.shape
    depth, cols = cen_ref.shape
    me = lax.axis_index("rows")
    my_group = lax.axis_index("cent")
    pos = position_of(me, ring)
    right = row_at((pos + 1) % ring, ring)
    left = row_at((pos + ring - 1) % ring, ring)
    neighbours = (right, left)
    chunks = min(4, cols // LANES)
    cw = cols // chunks

    barrier = pltpu.get_barrier_semaphore()

    def greet(o, carry):
        pl.semaphore_signal(barrier, inc=1, device_id={"rows": (me + o) % ring}, device_id_type=MESH)
        return carry

    lax.fori_loop(1, ring, greet, 0)
    for o in range(1, groups):
        pl.semaphore_signal(barrier, inc=1, device_id={"cent": (my_group + o) % groups}, device_id_type=MESH)

    tile = 256

    mine = pl.ds(pl.multiple_of(me * depth, depth), depth)
    cen_full[mine, :] = cen_ref[...]
    pl.semaphore_wait(barrier, ring - 1 + groups - 1)

    steps = (ring // 2, ring // 2 - 1)

    def gather_copy(way, step, chunk):
        source = (pos + ring - step) % ring if way == 0 else (pos + step) % ring
        block = row_at(source, ring)
        view = cen_full.at[pl.ds(pl.multiple_of(block * depth, depth), depth), pl.ds(chunk * cw, cw)]
        return pltpu.make_async_remote_copy(
            src_ref=view, dst_ref=view, send_sem=ag_send.at[way, step, chunk], recv_sem=ag_recv.at[way, step, chunk],
            device_id={"rows": neighbours[way]}, device_id_type=MESH)

    def gather_arrival(way, step, chunk):
        source = (pos + ring - step - 1) % ring if way == 0 else (pos + step + 1) % ring
        block = row_at(source, ring)
        view = cen_full.at[pl.ds(pl.multiple_of(block * depth, depth), depth), pl.ds(chunk * cw, cw)]
        return pltpu.make_async_remote_copy(
            src_ref=view, dst_ref=view, send_sem=ag_send.at[way, step, chunk], recv_sem=ag_recv.at[way, step, chunk],
            device_id={"rows": neighbours[way]}, device_id_type=MESH)

    for chunk in range(chunks):
        for way in range(2):
            gather_copy(way, 0, chunk).start()

    def turn(t, carry):
        at = pl.ds(pl.multiple_of(t * tile, tile), tile)
        vec_t[:, at] = vec_ref[at, :].T
        return carry

    lax.fori_loop(0, rows // tile, turn, 0)

    def gather_step(step, carry):
        for chunk in range(chunks):
            for way in range(2):
                gather_arrival(way, step - 1, chunk).wait_recv()
                gather_copy(way, step, chunk).start()
        return carry

    lax.fori_loop(1, steps[1], gather_step, 0)
    last = steps[1]
    for chunk in range(chunks):
        gather_arrival(0, last - 1, chunk).wait_recv()
        gather_copy(0, last, chunk).start()
        gather_arrival(1, last - 1, chunk).wait_recv()
    for chunk in range(chunks):
        gather_arrival(0, last, chunk).wait_recv()

    scale = SHARPNESS / math.sqrt(width)
    strips = cols // LANES

    def to_lanes(op):
        return op(part[...].T, axis=0, keepdims=True)

    def to_rows(vector):
        rows_b[...] = jnp.broadcast_to(vector, (LANES, rows)).T

    def score(t, carry):
        at = pl.ds(pl.multiple_of(t * tile, tile), tile)
        top = None
        for chunk in range(chunks):
            s = jnp.dot(vec_ref[at, :], cen_full[:, chunk * cw:(chunk + 1) * cw],
                        preferred_element_type=jnp.float32) * scale
            bal[at, chunk * cw:(chunk + 1) * cw] = s
            for j in range(cw // LANES):
                piece = s[:, j * LANES:(j + 1) * LANES]
                top = piece if top is None else jnp.maximum(top, piece)
        part[at, :] = jnp.broadcast_to(jnp.max(top, axis=1, keepdims=True), (tile, LANES))
        return carry

    lax.fori_loop(0, rows // tile, score, 0)
    top = to_lanes(jnp.max)
    row_x[0, 0, 0:1, :] = top

    small = 32

    def exponent(t, carry):
        at = pl.ds(pl.multiple_of(t * small, small), small)
        m = part[at, :]
        acc = None
        for j in range(strips):
            lanes = slice(j * LANES, (j + 1) * LANES)
            e = jnp.exp(bal[at, lanes] - m)
            bal[at, lanes] = e
            acc = e if acc is None else acc + e
        part[at, :] = acc
        return carry

    lax.fori_loop(0, rows // small, exponent, 0)
    row_x[0, 0, 1:2, :] = to_lanes(jnp.sum)

    def row_copy(turn_, o):
        return pltpu.make_async_remote_copy(
            src_ref=row_x.at[turn_, 0], dst_ref=row_x.at[turn_, o], send_sem=row_send.at[turn_, o],
            recv_sem=row_recv.at[turn_, o], device_id={"cent": (my_group + o) % groups}, device_id_type=MESH)

    def col_copy(turn_, o):
        return pltpu.make_async_remote_copy(
            src_ref=col_x.at[turn_, 0], dst_ref=col_x.at[turn_, o], send_sem=col_send.at[turn_, o],
            recv_sem=col_recv.at[turn_, o], device_id={"rows": (me + o) % ring}, device_id_type=MESH)

    def swap_rows(turn_):
        for o in range(1, groups):
            row_copy(turn_, o).start()
        for o in range(1, groups):
            row_copy(turn_, o).wait_recv()

    swap_rows(0)
    tops = [row_x[0, o, 0:1, :] for o in range(groups)]
    sums = [row_x[0, o, 1:2, :] for o in range(groups)]
    highest = functools.reduce(jnp.maximum, tops)
    total = functools.reduce(jnp.add, [s * jnp.exp(m - highest) for s, m in zip(sums, tops)])
    to_rows(jnp.exp(tops[0] - highest) / total)

    target = total_rows / columns_total

    def column_pass(column_scale):
        def body(t, accs):
            at = pl.ds(pl.multiple_of(t * small, small), small)
            r = rows_b[at, :]
            new = []
            for j in range(strips):
                lanes = slice(j * LANES, (j + 1) * LANES)
                b = bal[at, lanes]
                if column_scale is not None:
                    b = b * column_scale[:, lanes]
                b = b * r
                bal[at, lanes] = b
                folded = accs[j]
                for q in range(small // 8):
                    folded = folded + b[q * 8:(q + 1) * 8, :]
                new.append(folded)
            return tuple(new)

        accs = lax.fori_loop(0, rows // small, body, tuple(jnp.zeros((8, LANES), jnp.float32) for _ in range(strips)))
        return [jnp.sum(a, axis=0, keepdims=True) for a in accs]

    def row_pass(column_scale):
        def body(t, carry):
            at = pl.ds(pl.multiple_of(t * small, small), small)
            acc = None
            for j in range(strips):
                lanes = slice(j * LANES, (j + 1) * LANES)
                b = bal[at, lanes] * column_scale[:, lanes]
                acc = b if acc is None else acc + b
            part[at, :] = acc
            return carry

        lax.fori_loop(0, rows // small, body, 0)
        return to_lanes(jnp.sum)

    column_scale = None
    for it in range(ITERS):
        sums = column_pass(column_scale)
        for j in range(strips):
            col_x[it, 0, :, j * LANES:(j + 1) * LANES] = sums[j]

        def send(o, carry, it=it):
            col_copy(it, o).start()
            return carry

        def receive(o, acc, it=it):
            col_copy(it, o).wait_recv()
            return acc + col_x[it, o]

        lax.fori_loop(1, ring, send, 0)
        mass = lax.fori_loop(1, ring, receive, col_x[it, 0])
        column_scale = target / mass
        row_x[it + 1, 0, 0:1, :] = row_pass(column_scale)
        swap_rows(it + 1)
        mass = functools.reduce(jnp.add, [row_x[it + 1, o, 0:1, :] for o in range(groups)])
        to_rows(1.0 / mass)

    def weigh(t, carry):
        at = pl.ds(pl.multiple_of(t * small, small), small)
        r = rows_b[at, :]
        for j in range(strips):
            lanes = slice(j * LANES, (j + 1) * LANES)
            wts[at, lanes] = (bal[at, lanes] * column_scale[:, lanes] * r).astype(jnp.bfloat16)
        return carry

    lax.fori_loop(0, rows // small, weigh, 0)

    dt = min(256, width)
    factor = columns_total / total_rows

    def multiply(t, carry):
        at = pl.ds(pl.multiple_of(t * dt, dt), dt)
        for chunk in range(chunks):
            lanes = slice(chunk * cw, (chunk + 1) * cw)
            bal[at, lanes] = jnp.dot(vec_t[at, :], wts[:, lanes], preferred_element_type=jnp.float32) * factor
        return carry

    lax.fori_loop(0, width // dt, multiply, 0)

    def block_at(way, step):
        where = (pos + 2 * ring - 1 - step) % ring if way == 0 else (pos + 1 + step) % ring
        return pl.ds(pl.multiple_of(row_at(where, ring) * depth, depth), depth)

    pieces = chunks
    half = pieces // 2

    def sum_copy(piece, step):
        way = 0 if piece < half else 1
        lanes = pl.ds(piece * cw, cw)
        return pltpu.make_async_remote_copy(
            src_ref=bal.at[block_at(way, step), lanes], dst_ref=sum_in.at[step, piece],
            send_sem=rs_send.at[step, piece], recv_sem=rs_recv.at[step, piece],
            device_id={"rows": neighbours[way]}, device_id_type=MESH)

    order = [p + w * half for p in range(half) for w in range(2)]
    for piece in order:
        sum_copy(piece, 0).start()

    def sum_step(step, carry):
        for piece in order:
            way = 0 if piece < half else 1
            lanes = slice(piece * cw, (piece + 1) * cw)
            sum_copy(piece, step - 1).wait_recv()
            at = block_at(way, step)
            bal[at, lanes] = bal[at, lanes] + sum_in[step - 1, piece]
            sum_copy(piece, step).start()
        return carry

    lax.fori_loop(1, ring - 1, sum_step, 0)
    for piece in order:
        lanes = slice(piece * cw, (piece + 1) * cw)
        sum_copy(piece, ring - 2).wait_recv()
        out_ref[:, lanes] = bal[mine, lanes] + sum_in[ring - 2, piece]

    def drain_gather(step, carry):
        for chunk in range(chunks):
            for way in range(2):
                gather_copy(way, step, chunk).wait_send()
        return carry

    lax.fori_loop(0, steps[1], drain_gather, 0)
    for chunk in range(chunks):
        gather_copy(0, steps[1], chunk).wait_send()
    for turn_ in range(ITERS + 1):
        for o in range(1, groups):
            row_copy(turn_, o).wait_send()

    def drain_columns(o, carry):
        for it in range(ITERS):
            col_copy(it, o).wait_send()
        return carry

    lax.fori_loop(1, ring, drain_columns, 0)

    def drain_sums(step, carry):
        for piece in order:
            sum_copy(piece, step).wait_send()
        return carry

    lax.fori_loop(0, ring - 1, drain_sums, 0)


def solution(mesh):
    ring, groups = mesh.shape["rows"], mesh.shape["cent"]

    def on_device(vectors, centroids):
        rows, width = vectors.shape
        depth, cols = centroids.shape
        chunks = min(4, cols // LANES)
        f32, bf16 = jnp.float32, jnp.bfloat16
        dma = pltpu.SemaphoreType.DMA
        return pl.pallas_call(
            functools.partial(kernel, ring, groups, rows * ring, cols * groups),
            out_shape=jax.ShapeDtypeStruct((depth, cols), f32),
            in_specs=[pl.BlockSpec(memory_space=pltpu.VMEM)] * 2,
            out_specs=pl.BlockSpec(memory_space=pltpu.VMEM),
            scratch_shapes=[
                pltpu.VMEM((width, cols), bf16),
                pltpu.VMEM((width, rows), bf16),
                pltpu.VMEM((max(rows, width), cols), f32),
                pltpu.VMEM((rows, cols), bf16),
                pltpu.VMEM((rows, LANES), f32),
                pltpu.VMEM((rows, LANES), f32),
                pltpu.VMEM((ITERS + 1, groups, 2, rows), f32),
                pltpu.VMEM((ITERS, ring, 1, cols), f32),
                pltpu.VMEM((ring - 1, chunks, depth, cols // chunks), f32),
                dma((2, ring // 2, chunks)),
                dma((2, ring // 2, chunks)),
                dma((ITERS + 1, groups)),
                dma((ITERS + 1, groups)),
                dma((ITERS, ring)),
                dma((ITERS, ring)),
                dma((ring - 1, chunks)),
                dma((ring - 1, chunks)),
            ],
            compiler_params=pltpu.CompilerParams(
                collective_id=0, has_side_effects=True, vmem_limit_bytes=66 * 1000 * 1000),
        )(vectors, centroids)

    return jax.shard_map(
        on_device,
        mesh=mesh,
        in_specs=(P("rows", None), P("rows", "cent")),
        out_specs=P("rows", "cent"),
        check_vma=False,
    )
```

```python
import functools
import math

import jax
import jax.numpy as jnp
from jax import lax
from jax.experimental import pallas as pl
from jax.experimental.pallas import tpu as pltpu
from jax.sharding import PartitionSpec as P

ITERS = 3
SHARPNESS = 3.0
MESH = pl.DeviceIdType.MESH
LANES = 128
SHARES = 2


def short_steps(ring):
    steps = 0
    while (steps + 1) * (steps + 2) / 2 <= 0.65 * ring:
        steps += 1
    return steps


def position_of(row, ring):
    chips = ring // 2
    chip, core = row // 2, row % 2
    far, near = chip // 2, chip % 2
    place = far + near * (chips - 1 - 2 * far)
    return place * 2 + core


def row_at(position, ring):
    chips = ring // 2
    place, core = position // 2, position % 2
    half = chips // 2
    near = place // half
    far = place + near * (chips - 1 - 2 * place)
    return (far * 2 + near) * 2 + core


def kernel(ring, groups, shorts, total_rows, columns_total, vec_ref, cen_ref, out_ref, cen_full, vec_t, bal, wts, rows_b,
           part, row_x, col_x, short_out, short_in, sum_in, ag_send, ag_recv, row_send, row_recv, col_send, col_recv, rs_send, rs_recv):
    rows, width = vec_ref.shape
    depth, cols = cen_ref.shape
    me = lax.axis_index("rows")
    my_group = lax.axis_index("cent")
    pos = position_of(me, ring)
    right = row_at((pos + 1) % ring, ring)
    left = row_at((pos + ring - 1) % ring, ring)
    neighbours = (right, left)
    chunks = min(4, cols // LANES)
    cw = cols // chunks

    barrier = pltpu.get_barrier_semaphore()

    def greet(o, carry):
        pl.semaphore_signal(barrier, inc=1, device_id={"rows": (me + o) % ring}, device_id_type=MESH)
        return carry

    lax.fori_loop(1, ring, greet, 0)
    for o in range(1, groups):
        pl.semaphore_signal(barrier, inc=1, device_id={"cent": (my_group + o) % groups}, device_id_type=MESH)

    tile = 256

    mine = pl.ds(pl.multiple_of(me * depth, depth), depth)
    cen_full[mine, :] = cen_ref[...]
    pl.semaphore_wait(barrier, ring - 1 + groups - 1)

    steps = (ring // 2, ring // 2 - 1)

    def gather_copy(way, step, chunk):
        source = (pos + ring - step) % ring if way == 0 else (pos + step) % ring
        block = row_at(source, ring)
        view = cen_full.at[pl.ds(pl.multiple_of(block * depth, depth), depth), pl.ds(chunk * cw, cw)]
        return pltpu.make_async_remote_copy(
            src_ref=view, dst_ref=view, send_sem=ag_send.at[way, step, chunk], recv_sem=ag_recv.at[way, step, chunk],
            device_id={"rows": neighbours[way]}, device_id_type=MESH)

    def gather_arrival(way, step, chunk):
        source = (pos + ring - step - 1) % ring if way == 0 else (pos + step + 1) % ring
        block = row_at(source, ring)
        view = cen_full.at[pl.ds(pl.multiple_of(block * depth, depth), depth), pl.ds(chunk * cw, cw)]
        return pltpu.make_async_remote_copy(
            src_ref=view, dst_ref=view, send_sem=ag_send.at[way, step, chunk], recv_sem=ag_recv.at[way, step, chunk],
            device_id={"rows": neighbours[way]}, device_id_type=MESH)

    for chunk in range(chunks):
        for way in range(2):
            gather_copy(way, 0, chunk).start()

    def turn(t, carry):
        at = pl.ds(pl.multiple_of(t * tile, tile), tile)
        vec_t[:, at] = vec_ref[at, :].T
        return carry

    lax.fori_loop(0, rows // tile, turn, 0)

    def gather_step(step, carry):
        for chunk in range(chunks):
            for way in range(2):
                gather_arrival(way, step - 1, chunk).wait_recv()
                gather_copy(way, step, chunk).start()
        return carry

    lax.fori_loop(1, steps[1], gather_step, 0)
    last = steps[1]
    for chunk in range(chunks):
        gather_arrival(0, last - 1, chunk).wait_recv()
        gather_copy(0, last, chunk).start()
        gather_arrival(1, last - 1, chunk).wait_recv()
    for chunk in range(chunks):
        gather_arrival(0, last, chunk).wait_recv()

    scale = SHARPNESS / math.sqrt(width)
    strips = cols // LANES

    share = rows // SHARES

    def rows_of(part_):
        return pl.ds(part_ * share, share)

    def to_lanes(op, part_):
        return op(part[rows_of(part_), :].T, axis=0, keepdims=True)

    def to_rows(vector, part_):
        rows_b[rows_of(part_), :] = jnp.broadcast_to(vector, (LANES, share)).T

    def score(t, carry):
        at = pl.ds(pl.multiple_of(t * tile, tile), tile)
        top = None
        for chunk in range(chunks):
            s = jnp.dot(vec_ref[at, :], cen_full[:, chunk * cw:(chunk + 1) * cw],
                        preferred_element_type=jnp.float32) * scale
            bal[at, chunk * cw:(chunk + 1) * cw] = s
            for j in range(cw // LANES):
                piece = s[:, j * LANES:(j + 1) * LANES]
                top = piece if top is None else jnp.maximum(top, piece)
        part[at, :] = jnp.broadcast_to(jnp.max(top, axis=1, keepdims=True), (tile, LANES))
        return carry

    lax.fori_loop(0, rows // tile, score, 0)
    small = 32
    per_share = share // small

    def exponent(t, carry):
        at = pl.ds(pl.multiple_of(t * small, small), small)
        m = part[at, :]
        acc = None
        for j in range(strips):
            lanes = slice(j * LANES, (j + 1) * LANES)
            e = jnp.exp(bal[at, lanes] - m)
            bal[at, lanes] = e
            acc = e if acc is None else acc + e
        part[at, :] = acc
        return carry

    def row_copy(turn_, part_, o):
        return pltpu.make_async_remote_copy(
            src_ref=row_x.at[turn_, part_, 0], dst_ref=row_x.at[turn_, part_, o],
            send_sem=row_send.at[turn_, part_, o], recv_sem=row_recv.at[turn_, part_, o],
            device_id={"cent": (my_group + o) % groups}, device_id_type=MESH)

    def col_copy(turn_, o):
        return pltpu.make_async_remote_copy(
            src_ref=col_x.at[turn_, 0], dst_ref=col_x.at[turn_, o], send_sem=col_send.at[turn_, o],
            recv_sem=col_recv.at[turn_, o], device_id={"rows": (me + o) % ring}, device_id_type=MESH)

    def send_rows(turn_, part_):
        for o in range(1, groups):
            row_copy(turn_, part_, o).start()

    def receive_rows(turn_, part_):
        for o in range(1, groups):
            row_copy(turn_, part_, o).wait_recv()

    for part_ in range(SHARES):
        row_x[0, part_, 0, 0:1, :] = to_lanes(jnp.max, part_)
        lax.fori_loop(part_ * per_share, (part_ + 1) * per_share, exponent, 0)
        row_x[0, part_, 0, 1:2, :] = to_lanes(jnp.sum, part_)
        send_rows(0, part_)

    def softmax_rows(part_):
        receive_rows(0, part_)
        tops = [row_x[0, part_, o, 0:1, :] for o in range(groups)]
        sums = [row_x[0, part_, o, 1:2, :] for o in range(groups)]
        highest = functools.reduce(jnp.maximum, tops)
        total = functools.reduce(jnp.add, [s * jnp.exp(m - highest) for s, m in zip(sums, tops)])
        to_rows(jnp.exp(tops[0] - highest) / total, part_)

    def balance_rows(turn_, part_):
        receive_rows(turn_, part_)
        mass = functools.reduce(jnp.add, [row_x[turn_, part_, o, 0:1, :] for o in range(groups)])
        to_rows(1.0 / mass, part_)

    target = total_rows / columns_total

    def column_pass(column_scale, part_, accs):
        def body(t, accs):
            at = pl.ds(pl.multiple_of(t * small, small), small)
            r = rows_b[at, :]
            new = []
            for j in range(strips):
                lanes = slice(j * LANES, (j + 1) * LANES)
                b = bal[at, lanes]
                if column_scale is not None:
                    b = b * column_scale[:, lanes]
                b = b * r
                bal[at, lanes] = b
                folded = accs[j]
                for q in range(small // 8):
                    folded = folded + b[q * 8:(q + 1) * 8, :]
                new.append(folded)
            return tuple(new)

        return lax.fori_loop(part_ * per_share, (part_ + 1) * per_share, body, accs)

    def row_pass(column_scale, part_):
        def body(t, carry):
            at = pl.ds(pl.multiple_of(t * small, small), small)
            acc = None
            for j in range(strips):
                lanes = slice(j * LANES, (j + 1) * LANES)
                b = bal[at, lanes] * column_scale[:, lanes]
                acc = b if acc is None else acc + b
            part[at, :] = acc
            return carry

        lax.fori_loop(part_ * per_share, (part_ + 1) * per_share, body, 0)
        return to_lanes(jnp.sum, part_)

    column_scale = None
    for it in range(ITERS):
        accs = tuple(jnp.zeros((8, LANES), jnp.float32) for _ in range(strips))
        for part_ in range(SHARES):
            if it == 0:
                softmax_rows(part_)
            else:
                balance_rows(it, part_)
            accs = column_pass(column_scale, part_, accs)
        for j in range(strips):
            col_x[it, 0, :, j * LANES:(j + 1) * LANES] = jnp.sum(accs[j], axis=0, keepdims=True)

        def send(o, carry, it=it):
            col_copy(it, o).start()
            return carry

        def receive(o, acc, it=it):
            col_copy(it, o).wait_recv()
            return acc + col_x[it, o]

        lax.fori_loop(1, ring, send, 0)
        mass = lax.fori_loop(1, ring, receive, col_x[it, 0])
        column_scale = target / mass
        for part_ in range(SHARES):
            row_x[it + 1, part_, 0, 0:1, :] = row_pass(column_scale, part_)
            send_rows(it + 1, part_)

    def weigh(t, carry):
        at = pl.ds(pl.multiple_of(t * small, small), small)
        r = rows_b[at, :]
        for j in range(strips):
            lanes = slice(j * LANES, (j + 1) * LANES)
            wts[at, lanes] = (bal[at, lanes] * column_scale[:, lanes] * r).astype(jnp.bfloat16)
        return carry

    for part_ in range(SHARES):
        balance_rows(ITERS, part_)
        lax.fori_loop(part_ * per_share, (part_ + 1) * per_share, weigh, 0)

    dt = min(256, width)
    factor = columns_total / total_rows

    def block_at(way, step):
        where = (pos + 2 * ring - 1 - step) % ring if way == 0 else (pos + 1 + step) % ring
        return pl.ds(pl.multiple_of(row_at(where, ring) * depth, depth), depth)

    pieces = chunks
    half = pieces // 2

    def sum_copy(piece, step):
        way = 0 if piece < half else 1
        lanes = pl.ds(piece * cw, cw)
        if step < shorts:
            source, target_ = short_out.at[step, piece], short_in.at[step, piece]
        else:
            source, target_ = bal.at[block_at(way, step), lanes], sum_in.at[step - shorts, piece]
        return pltpu.make_async_remote_copy(
            src_ref=source, dst_ref=target_, send_sem=rs_send.at[step, piece], recv_sem=rs_recv.at[step, piece],
            device_id={"rows": neighbours[way]}, device_id_type=MESH)

    def arrived(piece, step):
        if step < shorts:
            return short_in[step, piece].astype(jnp.float32)
        return sum_in[step - shorts, piece]

    def advance(piece, step):
        way = 0 if piece < half else 1
        lanes = slice(piece * cw, (piece + 1) * cw)
        at = mine if step == ring - 1 else block_at(way, step)
        value = bal[at, lanes]
        if step > 0:
            sum_copy(piece, step - 1).wait_recv()
            value = value + arrived(piece, step - 1)
        if step == ring - 1:
            out_ref[:, lanes] = value
            return
        if step < shorts:
            short_out[step, piece] = value.astype(jnp.bfloat16)
        elif step > 0:
            bal[at, lanes] = value
        sum_copy(piece, step).start()

    order = [p + w * half for p in range(half) for w in range(2)]
    done = {}
    tiles = width // dt
    for piece in order:
        lanes = slice(piece * cw, (piece + 1) * cw)

        def multiply(t, carry, lanes=lanes):
            at = pl.ds(pl.multiple_of(t * dt, dt), dt)
            bal[at, lanes] = jnp.dot(vec_t[at, :], wts[:, lanes], preferred_element_type=jnp.float32) * factor
            return carry

        for first in range(0, tiles, 2):
            lax.fori_loop(first, min(first + 2, tiles), multiply, 0)
            for other in done:
                if done[other] < ring - 1:
                    advance(other, done[other])
                    done[other] += 1
        advance(piece, 0)
        done[piece] = 1
    while min(done.values()) < ring:
        for piece in order:
            if done[piece] < ring:
                advance(piece, done[piece])
                done[piece] += 1

    def drain_gather(step, carry):
        for chunk in range(chunks):
            for way in range(2):
                gather_copy(way, step, chunk).wait_send()
        return carry

    lax.fori_loop(0, steps[1], drain_gather, 0)
    for chunk in range(chunks):
        gather_copy(0, steps[1], chunk).wait_send()
    for turn_ in range(ITERS + 1):
        for part_ in range(SHARES):
            for o in range(1, groups):
                row_copy(turn_, part_, o).wait_send()

    def drain_columns(o, carry):
        for it in range(ITERS):
            col_copy(it, o).wait_send()
        return carry

    lax.fori_loop(1, ring, drain_columns, 0)

    for step in range(ring - 1):
        for piece in order:
            sum_copy(piece, step).wait_send()


def solution(mesh):
    ring, groups = mesh.shape["rows"], mesh.shape["cent"]

    def on_device(vectors, centroids):
        rows, width = vectors.shape
        depth, cols = centroids.shape
        chunks = min(4, cols // LANES)
        shorts = short_steps(ring)
        f32, bf16 = jnp.float32, jnp.bfloat16
        dma = pltpu.SemaphoreType.DMA
        return pl.pallas_call(
            functools.partial(kernel, ring, groups, shorts, rows * ring, cols * groups),
            out_shape=jax.ShapeDtypeStruct((depth, cols), f32),
            in_specs=[pl.BlockSpec(memory_space=pltpu.VMEM)] * 2,
            out_specs=pl.BlockSpec(memory_space=pltpu.VMEM),
            scratch_shapes=[
                pltpu.VMEM((width, cols), bf16),
                pltpu.VMEM((width, rows), bf16),
                pltpu.VMEM((max(rows, width), cols), f32),
                pltpu.VMEM((rows, cols), bf16),
                pltpu.VMEM((rows, LANES), f32),
                pltpu.VMEM((rows, LANES), f32),
                pltpu.VMEM((ITERS + 1, SHARES, groups, 2, rows // SHARES), f32),
                pltpu.VMEM((ITERS, ring, 1, cols), f32),
                pltpu.VMEM((shorts, chunks, depth, cols // chunks), bf16),
                pltpu.VMEM((shorts, chunks, depth, cols // chunks), bf16),
                pltpu.VMEM((ring - 1 - shorts, chunks, depth, cols // chunks), f32),
                dma((2, ring // 2, chunks)),
                dma((2, ring // 2, chunks)),
                dma((ITERS + 1, SHARES, groups)),
                dma((ITERS + 1, SHARES, groups)),
                dma((ITERS, ring)),
                dma((ITERS, ring)),
                dma((ring - 1, chunks)),
                dma((ring - 1, chunks)),
            ],
            compiler_params=pltpu.CompilerParams(
                collective_id=0, has_side_effects=True, vmem_limit_bytes=66 * 1000 * 1000),
        )(vectors, centroids)

    return jax.shard_map(
        on_device,
        mesh=mesh,
        in_specs=(P("rows", None), P("rows", "cent")),
        out_specs=P("rows", "cent"),
        check_vma=False,
    )
```

```python
import functools
import math

import jax
import jax.numpy as jnp
from jax import lax
from jax.experimental import pallas as pl
from jax.experimental.pallas import tpu as pltpu
from jax.sharding import PartitionSpec as P

ITERS = 3
SHARPNESS = 3.0
MESH = pl.DeviceIdType.MESH
LANES = 128
SHARES = 2


def short_steps(ring):
    steps = 0
    while (steps + 1) * (steps + 2) / 2 <= 0.65 * ring:
        steps += 1
    return steps


def position_of(row, ring):
    chips = ring // 2
    chip, core = row // 2, row % 2
    far, near = chip // 2, chip % 2
    place = far + near * (chips - 1 - 2 * far)
    return place * 2 + core


def row_at(position, ring):
    chips = ring // 2
    place, core = position // 2, position % 2
    half = chips // 2
    near = place // half
    far = place + near * (chips - 1 - 2 * place)
    return (far * 2 + near) * 2 + core


def kernel(ring, groups, shorts, total_rows, columns_total, vec_ref, cen_ref, out_ref, cen_full, vec_t, bal, wts, rows_b,
           part, row_x, col_x, short_out, short_in, sum_in, ag_send, ag_recv, row_send, row_recv, col_send, col_recv, rs_send, rs_recv):
    rows, width = vec_ref.shape
    depth, cols = cen_ref.shape
    me = lax.axis_index("rows")
    my_group = lax.axis_index("cent")
    pos = position_of(me, ring)
    right = row_at((pos + 1) % ring, ring)
    left = row_at((pos + ring - 1) % ring, ring)
    neighbours = (right, left)
    chunks = min(4, cols // LANES)
    cw = cols // chunks

    barrier = pltpu.get_barrier_semaphore()

    def greet(o, carry):
        pl.semaphore_signal(barrier, inc=1, device_id={"rows": (me + o) % ring}, device_id_type=MESH)
        return carry

    lax.fori_loop(1, ring, greet, 0)
    for o in range(1, groups):
        pl.semaphore_signal(barrier, inc=1, device_id={"cent": (my_group + o) % groups}, device_id_type=MESH)

    tile = 256

    mine = pl.ds(pl.multiple_of(me * depth, depth), depth)
    cen_full[mine, :] = cen_ref[...]
    pl.semaphore_wait(barrier, ring - 1 + groups - 1)

    steps = (ring // 2, ring // 2 - 1)

    def gather_copy(way, step, chunk):
        source = (pos + ring - step) % ring if way == 0 else (pos + step) % ring
        block = row_at(source, ring)
        view = cen_full.at[pl.ds(pl.multiple_of(block * depth, depth), depth), pl.ds(chunk * cw, cw)]
        return pltpu.make_async_remote_copy(
            src_ref=view, dst_ref=view, send_sem=ag_send.at[way, step, chunk], recv_sem=ag_recv.at[way, step, chunk],
            device_id={"rows": neighbours[way]}, device_id_type=MESH)

    def gather_arrival(way, step, chunk):
        source = (pos + ring - step - 1) % ring if way == 0 else (pos + step + 1) % ring
        block = row_at(source, ring)
        view = cen_full.at[pl.ds(pl.multiple_of(block * depth, depth), depth), pl.ds(chunk * cw, cw)]
        return pltpu.make_async_remote_copy(
            src_ref=view, dst_ref=view, send_sem=ag_send.at[way, step, chunk], recv_sem=ag_recv.at[way, step, chunk],
            device_id={"rows": neighbours[way]}, device_id_type=MESH)

    for chunk in range(chunks):
        for way in range(2):
            gather_copy(way, 0, chunk).start()

    def turn(t, carry):
        at = pl.ds(pl.multiple_of(t * tile, tile), tile)
        vec_t[:, at] = vec_ref[at, :].T
        return carry

    lax.fori_loop(0, rows // tile, turn, 0)

    def gather_step(step, carry):
        for chunk in range(chunks):
            for way in range(2):
                gather_arrival(way, step - 1, chunk).wait_recv()
                gather_copy(way, step, chunk).start()
        return carry

    lax.fori_loop(1, steps[1], gather_step, 0)
    last = steps[1]
    for chunk in range(chunks):
        gather_arrival(0, last - 1, chunk).wait_recv()
        gather_copy(0, last, chunk).start()
        gather_arrival(1, last - 1, chunk).wait_recv()
    for chunk in range(chunks):
        gather_arrival(0, last, chunk).wait_recv()

    scale = SHARPNESS / math.sqrt(width)
    strips = cols // LANES

    share = rows // SHARES

    def rows_of(part_):
        return pl.ds(part_ * share, share)

    def to_lanes(op, part_):
        return op(part[rows_of(part_), :].T, axis=0, keepdims=True)

    def to_rows(vector, part_):
        rows_b[rows_of(part_), :] = jnp.broadcast_to(vector, (LANES, share)).T

    def score(t, carry):
        at = pl.ds(pl.multiple_of(t * tile, tile), tile)
        top = None
        for chunk in range(chunks):
            s = jnp.dot(vec_ref[at, :], cen_full[:, chunk * cw:(chunk + 1) * cw],
                        preferred_element_type=jnp.float32) * scale
            bal[at, chunk * cw:(chunk + 1) * cw] = s
            for j in range(cw // LANES):
                piece = s[:, j * LANES:(j + 1) * LANES]
                top = piece if top is None else jnp.maximum(top, piece)
        part[at, :] = jnp.broadcast_to(jnp.max(top, axis=1, keepdims=True), (tile, LANES))
        return carry

    lax.fori_loop(0, rows // tile, score, 0)
    small = 32
    per_share = share // small

    def exponent(t, carry):
        at = pl.ds(pl.multiple_of(t * small, small), small)
        m = part[at, :]
        acc = None
        for j in range(strips):
            lanes = slice(j * LANES, (j + 1) * LANES)
            e = jnp.exp(bal[at, lanes] - m)
            bal[at, lanes] = e
            acc = e if acc is None else acc + e
        part[at, :] = acc
        return carry

    def row_copy(turn_, part_, o):
        return pltpu.make_async_remote_copy(
            src_ref=row_x.at[turn_, part_, 0], dst_ref=row_x.at[turn_, part_, o],
            send_sem=row_send.at[turn_, part_, o], recv_sem=row_recv.at[turn_, part_, o],
            device_id={"cent": (my_group + o) % groups}, device_id_type=MESH)

    def col_copy(turn_, o):
        return pltpu.make_async_remote_copy(
            src_ref=col_x.at[turn_, 0], dst_ref=col_x.at[turn_, o], send_sem=col_send.at[turn_, o],
            recv_sem=col_recv.at[turn_, o], device_id={"rows": (me + o) % ring}, device_id_type=MESH)

    def send_rows(turn_, part_):
        for o in range(1, groups):
            row_copy(turn_, part_, o).start()

    def receive_rows(turn_, part_):
        for o in range(1, groups):
            row_copy(turn_, part_, o).wait_recv()

    for part_ in range(SHARES):
        row_x[0, part_, 0, 0:1, :] = to_lanes(jnp.max, part_)
        lax.fori_loop(part_ * per_share, (part_ + 1) * per_share, exponent, 0)
        row_x[0, part_, 0, 1:2, :] = to_lanes(jnp.sum, part_)
        send_rows(0, part_)

    def softmax_rows(part_):
        receive_rows(0, part_)
        tops = [row_x[0, part_, o, 0:1, :] for o in range(groups)]
        sums = [row_x[0, part_, o, 1:2, :] for o in range(groups)]
        highest = functools.reduce(jnp.maximum, tops)
        total = functools.reduce(jnp.add, [s * jnp.exp(m - highest) for s, m in zip(sums, tops)])
        to_rows(jnp.exp(tops[0] - highest) / total, part_)

    def balance_rows(turn_, part_):
        receive_rows(turn_, part_)
        mass = functools.reduce(jnp.add, [row_x[turn_, part_, o, 0:1, :] for o in range(groups)])
        to_rows(1.0 / mass, part_)

    target = total_rows / columns_total

    def column_pass(column_scale, part_, accs):
        def body(t, accs):
            at = pl.ds(pl.multiple_of(t * small, small), small)
            r = rows_b[at, :]
            new = []
            for j in range(strips):
                lanes = slice(j * LANES, (j + 1) * LANES)
                b = bal[at, lanes]
                if column_scale is not None:
                    b = b * column_scale[:, lanes]
                b = b * r
                bal[at, lanes] = b
                folded = accs[j]
                for q in range(small // 8):
                    folded = folded + b[q * 8:(q + 1) * 8, :]
                new.append(folded)
            return tuple(new)

        return lax.fori_loop(part_ * per_share, (part_ + 1) * per_share, body, accs)

    def row_pass(column_scale, part_):
        def body(t, carry):
            at = pl.ds(pl.multiple_of(t * small, small), small)
            acc = None
            for j in range(strips):
                lanes = slice(j * LANES, (j + 1) * LANES)
                b = bal[at, lanes] * column_scale[:, lanes]
                acc = b if acc is None else acc + b
            part[at, :] = acc
            return carry

        lax.fori_loop(part_ * per_share, (part_ + 1) * per_share, body, 0)
        return to_lanes(jnp.sum, part_)

    column_scale = None
    for it in range(ITERS):
        accs = tuple(jnp.zeros((8, LANES), jnp.float32) for _ in range(strips))
        for part_ in range(SHARES):
            if it == 0:
                softmax_rows(part_)
            else:
                balance_rows(it, part_)
            accs = column_pass(column_scale, part_, accs)
        for j in range(strips):
            col_x[it, 0, :, j * LANES:(j + 1) * LANES] = jnp.sum(accs[j], axis=0, keepdims=True)

        def send(o, carry, it=it):
            col_copy(it, o).start()
            return carry

        def receive(o, acc, it=it):
            col_copy(it, o).wait_recv()
            return acc + col_x[it, o]

        lax.fori_loop(1, ring, send, 0)
        mass = lax.fori_loop(1, ring, receive, col_x[it, 0])
        column_scale = target / mass
        for part_ in range(SHARES):
            row_x[it + 1, part_, 0, 0:1, :] = row_pass(column_scale, part_)
            send_rows(it + 1, part_)

    def weigh(t, carry):
        at = pl.ds(pl.multiple_of(t * small, small), small)
        r = rows_b[at, :]
        for j in range(strips):
            lanes = slice(j * LANES, (j + 1) * LANES)
            wts[at, lanes] = (bal[at, lanes] * column_scale[:, lanes] * r).astype(jnp.bfloat16)
        return carry

    for part_ in range(SHARES):
        balance_rows(ITERS, part_)
        lax.fori_loop(part_ * per_share, (part_ + 1) * per_share, weigh, 0)

    dt = min(256, width)
    factor = columns_total / total_rows

    def block_at(way, step):
        where = (pos + 2 * ring - 1 - step) % ring if way == 0 else (pos + 1 + step) % ring
        return pl.ds(pl.multiple_of(row_at(where, ring) * depth, depth), depth)

    pieces = chunks
    half = pieces // 2

    def sum_copy(piece, step):
        way = 0 if piece < half else 1
        lanes = pl.ds(piece * cw, cw)
        if step < shorts:
            source, target_ = short_out.at[step, piece], short_in.at[step, piece]
        else:
            source, target_ = bal.at[block_at(way, step), lanes], sum_in.at[step - shorts, piece]
        return pltpu.make_async_remote_copy(
            src_ref=source, dst_ref=target_, send_sem=rs_send.at[step, piece], recv_sem=rs_recv.at[step, piece],
            device_id={"rows": neighbours[way]}, device_id_type=MESH)

    def arrived(piece, step):
        if step < shorts:
            return short_in[step, piece].astype(jnp.float32)
        return sum_in[step - shorts, piece]

    def advance(piece, step):
        way = 0 if piece < half else 1
        lanes = slice(piece * cw, (piece + 1) * cw)
        at = mine if step == ring - 1 else block_at(way, step)
        value = bal[at, lanes]
        if step > 0:
            sum_copy(piece, step - 1).wait_recv()
            value = value + arrived(piece, step - 1)
        if step == ring - 1:
            out_ref[:, lanes] = value
            return
        if step < shorts:
            short_out[step, piece] = value.astype(jnp.bfloat16)
        elif step > 0:
            bal[at, lanes] = value
        sum_copy(piece, step).start()

    order = [p + w * half for p in range(half) for w in range(2)]
    done = {}
    tiles = width // dt
    for piece in order:
        lanes = slice(piece * cw, (piece + 1) * cw)

        def multiply(t, carry, lanes=lanes):
            at = pl.ds(pl.multiple_of(t * dt, dt), dt)
            bal[at, lanes] = jnp.dot(vec_t[at, :], wts[:, lanes], preferred_element_type=jnp.float32) * factor
            return carry

        lax.fori_loop(0, tiles, multiply, 0)
        advance(piece, 0)
        done[piece] = 1
    while min(done.values()) < ring:
        for piece in order:
            if done[piece] < ring:
                advance(piece, done[piece])
                done[piece] += 1

    def drain_gather(step, carry):
        for chunk in range(chunks):
            for way in range(2):
                gather_copy(way, step, chunk).wait_send()
        return carry

    lax.fori_loop(0, steps[1], drain_gather, 0)
    for chunk in range(chunks):
        gather_copy(0, steps[1], chunk).wait_send()
    for turn_ in range(ITERS + 1):
        for part_ in range(SHARES):
            for o in range(1, groups):
                row_copy(turn_, part_, o).wait_send()

    def drain_columns(o, carry):
        for it in range(ITERS):
            col_copy(it, o).wait_send()
        return carry

    lax.fori_loop(1, ring, drain_columns, 0)

    for step in range(ring - 1):
        for piece in order:
            sum_copy(piece, step).wait_send()


def solution(mesh):
    ring, groups = mesh.shape["rows"], mesh.shape["cent"]

    def on_device(vectors, centroids):
        rows, width = vectors.shape
        depth, cols = centroids.shape
        chunks = min(4, cols // LANES)
        shorts = short_steps(ring)
        f32, bf16 = jnp.float32, jnp.bfloat16
        dma = pltpu.SemaphoreType.DMA
        return pl.pallas_call(
            functools.partial(kernel, ring, groups, shorts, rows * ring, cols * groups),
            out_shape=jax.ShapeDtypeStruct((depth, cols), f32),
            in_specs=[pl.BlockSpec(memory_space=pltpu.VMEM)] * 2,
            out_specs=pl.BlockSpec(memory_space=pltpu.VMEM),
            scratch_shapes=[
                pltpu.VMEM((width, cols), bf16),
                pltpu.VMEM((width, rows), bf16),
                pltpu.VMEM((max(rows, width), cols), f32),
                pltpu.VMEM((rows, cols), bf16),
                pltpu.VMEM((rows, LANES), f32),
                pltpu.VMEM((rows, LANES), f32),
                pltpu.VMEM((ITERS + 1, SHARES, groups, 2, rows // SHARES), f32),
                pltpu.VMEM((ITERS, ring, 1, cols), f32),
                pltpu.VMEM((shorts, chunks, depth, cols // chunks), bf16),
                pltpu.VMEM((shorts, chunks, depth, cols // chunks), bf16),
                pltpu.VMEM((ring - 1 - shorts, chunks, depth, cols // chunks), f32),
                dma((2, ring // 2, chunks)),
                dma((2, ring // 2, chunks)),
                dma((ITERS + 1, SHARES, groups)),
                dma((ITERS + 1, SHARES, groups)),
                dma((ITERS, ring)),
                dma((ITERS, ring)),
                dma((ring - 1, chunks)),
                dma((ring - 1, chunks)),
            ],
            compiler_params=pltpu.CompilerParams(
                collective_id=0, has_side_effects=True, vmem_limit_bytes=66 * 1000 * 1000),
        )(vectors, centroids)

    return jax.shard_map(
        on_device,
        mesh=mesh,
        in_specs=(P("rows", None), P("rows", "cent")),
        out_specs=P("rows", "cent"),
        check_vma=False,
    )
```
